256 devices in a mesh: dp: 4 (over x_lo, core), sp: 64 (over x_hi, z, y).
Axes of the slice: x: 4 (x_hi: 2, x_lo: 2; x = x_hi * 2 + x_lo), y: 4, z: 8, core: 2. Of those that a mesh axis runs over, the one named last changes fastest.
Arguments:
- ssm_input: bfloat16 [4, 8192, 8192], P('dp', 'sp'), may hold values from -6 to 6
- b_input: bfloat16 [4, 8192, 1024], P('dp', 'sp'), may hold values from -6 to 6
- c_input: bfloat16 [4, 8192, 1024], P('dp', 'sp'), may hold values from -6 to 6
- dt_input: bfloat16 [4, 8192, 128], P('dp', 'sp'), may hold values from -4 to 4
- conv_weight: float32 [4, 10240], replicated, may hold values from -3 to 3
- conv_bias: float32 [10240], replicated, may hold values from -3 to 3
- a_log: float32 [128], replicated, may hold values from -12 to 2
- dt_bias: float32 [128], replicated, may hold values from -5 to -3
- skip_gain: float32 [128], replicated, may hold values from 0.5 to 1.5
- grad_out: bfloat16 [4, 8192, 8192], P('dp', 'sp'), may hold values from -6 to 6
Outputs:
- y_out: bfloat16 [4, 8192, 8192], P('dp', 'sp')
- grad_x: bfloat16 [4, 8192, 8192], P('dp', 'sp')
- grad_b: bfloat16 [4, 8192, 1024], P('dp', 'sp')
- grad_c: bfloat16 [4, 8192, 1024], P('dp', 'sp')
- grad_dt: bfloat16 [4, 8192, 128], P('dp', 'sp')
- grad_conv_w: float32 [4, 10240], replicated
- grad_conv_b: float32 [10240], replicated
- grad_heads: float32 [3, 128], P(None, 'sp')
The draws below stay inside these ranges and needn't reach their ends.
All inputs are finite; a program needn't handle non-finite values.
Results may differ from the reference program's by a relative error of at most 0.015.
Values may be sent and summed in bfloat16 or wider, within the bound.
A program may use at most 192 MiB of HBM per device.

```python
import jax
import jax.numpy as jnp
from jax import lax

H = 128
P_SIZE = 64
N = 256
G = 4
K = 4
Q = 128
LEN = 8192
SEQS = 4
CH = 10240
N_SP = 64


def draw_a_log(key, part):
    pick_key, fast_key, slow_key = jax.random.split(key, 3)
    fast_share = 0.5
    chosen = jax.random.uniform(pick_key, (H,), jnp.float32) < fast_share
    fast_rate = 1.0 / jax.random.uniform(fast_key, (H,), jnp.float32, minval=30.0, maxval=50.0)
    slow_rate = jax.random.uniform(slow_key, (H,), jnp.float32, minval=0.3, maxval=2.0) / LEN
    chosen_rate = jnp.where(chosen, fast_rate, slow_rate)
    return jnp.log(chosen_rate / 0.02).astype(jnp.float32)


def steps_of(key, extent, cuts, low, top_value):
    def one(axis_at, blocks):
        steps = jax.random.uniform(jax.random.fold_in(jax.random.fold_in(key, 6), axis_at), (blocks,), jnp.float32, low / len(cuts), top_value / len(cuts))
        return jnp.repeat(jnp.exp(steps), extent[axis_at] // blocks).reshape((-1,) + (1,) * (len(extent) - axis_at - 1))

    gain = one(*cuts[0])
    for cut in cuts[1:]:
        gain = gain * one(*cut)
    return gain


def normal_values(own_key, dims, spread, most, cuts=(), kind=jnp.bfloat16):
    gain = steps_of(own_key, dims, cuts, -0.22, 0.18) if cuts else 1.0
    result = jax.random.normal(own_key, dims, jnp.float32) * spread * gain
    return jnp.minimum(jnp.maximum(result, -most), most).astype(kind)


def setup_inputs(seed: int = 0) -> dict:
    keys = jax.random.split(jax.random.key(seed), 11)
    ssm_input = normal_values(keys[0], (SEQS, LEN, H * P_SIZE), 1.0, 6.0, ((0, 4), (1, 64)))
    b_input = normal_values(keys[1], (SEQS, LEN, G * N), 1.0, 6.0, ((0, 4), (1, 64)))
    c_input = normal_values(keys[2], (SEQS, LEN, G * N), 1.0, 6.0, ((0, 4), (1, 64)))
    dt_input = normal_values(keys[3], (SEQS, LEN, H), 1.0, 4.0, ((0, 4), (1, 64)))
    conv_weight = normal_values(keys[4], (K, CH), K ** -0.5, 3.0, (), jnp.float32)
    conv_bias = normal_values(keys[5], (CH,), 0.5, 3.0, (), jnp.float32)
    a_log = draw_a_log(jax.random.fold_in(keys[10], 71), 0)
    dt_bias = jnp.clip(jax.random.uniform(keys[7], (H,), jnp.float32, -5.0, -3.0), -5.0, -3.0)
    skip_gain = jnp.clip(jax.random.uniform(keys[8], (H,), jnp.float32, 0.5, 1.5), 0.5, 1.5)
    grad_out = normal_values(keys[9], (SEQS, LEN, H * P_SIZE), 1.0, 6.0, ((0, 4), (1, 64)))
    return dict(ssm_input=ssm_input, b_input=b_input, c_input=c_input, dt_input=dt_input, conv_weight=conv_weight, conv_bias=conv_bias, a_log=a_log, dt_bias=dt_bias, skip_gain=skip_gain, grad_out=grad_out)


def conv_silu(padded, kernel_cols, offset_cols):
    span = kernel_cols.shape[0]
    count_rows = padded.shape[0] - span + 1
    summed = offset_cols[None, :] + jnp.zeros((count_rows, offset_cols.shape[0]), jnp.float32)
    for tap_index in range(span):
        summed = summed + kernel_cols[tap_index][None, :] * padded[tap_index:tap_index + count_rows]
    return jax.nn.silu(summed)

def conv_all(x_full, b_full, c_full, kernel, offset):
    x_width = x_full.shape[1]
    b_width = b_full.shape[1]
    x_out = conv_silu(x_full, kernel[:, :x_width], offset[:x_width])
    b_out = conv_silu(b_full, kernel[:, x_width:x_width + b_width], offset[x_width:x_width + b_width])
    c_out = conv_silu(c_full, kernel[:, x_width + b_width:], offset[x_width + b_width:])
    return (x_out, b_out, c_out)

def product(form, left, right):
    return jnp.einsum(form, left.astype(jnp.float32), right.astype(jnp.float32), precision=lax.Precision.HIGHEST)

def ssd_block(x_heads, dt_heads, b_group, c_group, alog_heads, dtbias_heads, skip_heads):
    length = x_heads.shape[0]
    nheads = dt_heads.shape[1]
    states = b_group.shape[1]
    hwidth = x_heads.shape[1] // nheads
    blocks = length // Q
    step_size = jax.nn.softplus(dt_heads.astype(jnp.float32) + dtbias_heads[None, :])
    steps_t = jnp.transpose(step_size).reshape(nheads, blocks, Q)
    log_t = steps_t * (-jnp.exp(alog_heads))[:, None, None]
    running = jnp.cumsum(log_t, axis=2)
    x_blocks = x_heads.reshape(blocks, Q, nheads * hwidth)
    b_blocks = b_group.reshape(blocks, Q, states)
    c_blocks = c_group.reshape(blocks, Q, states)
    scores = product('cqn,ckn->cqk', c_blocks, b_blocks)
    causal = (jnp.arange(Q)[:, None] >= jnp.arange(Q)[None, :])[None, None, :, :]
    spread_log = jnp.where(causal, running[:, :, :, None] - running[:, :, None, :], -1e+30)
    mixing = (scores[None] * jnp.exp(spread_log) * steps_t[:, :, None, :]).astype(jnp.bfloat16)
    within = product('hcqk,ckhp->cqhp', mixing, x_blocks.reshape(blocks, Q, nheads, hwidth))
    to_end = jnp.exp(running[:, :, -1:] - running)
    factor = jnp.transpose(steps_t * to_end, (1, 2, 0))
    x_wide = x_blocks.astype(jnp.float32).reshape(blocks, Q, nheads, hwidth)
    weighted = (x_wide * factor[:, :, :, None]).astype(jnp.bfloat16).reshape(blocks, Q, nheads * hwidth)
    block_states = product('ckn,ckm->cnm', b_blocks, weighted)
    totals = running[:, :, -1]
    before = jnp.cumsum(totals, axis=1) - totals
    earlier = (jnp.arange(blocks)[:, None] > jnp.arange(blocks)[None, :])[None, :, :]
    gap_log = jnp.where(earlier, before[:, :, None] - before[:, None, :] - totals[:, None, :], -1e+30)
    carried = jnp.exp(gap_log)
    entering = jnp.einsum('hcd,dnhp->cnhp', carried, block_states.reshape(blocks, states, nheads, hwidth), precision=lax.Precision.HIGHEST)
    entering_low = entering.reshape(blocks, states, nheads * hwidth).astype(jnp.bfloat16)
    across = product('cqn,cnm->cqm', c_blocks, entering_low).reshape(blocks, Q, nheads, hwidth)
    across = across * jnp.transpose(jnp.exp(running), (1, 2, 0))[:, :, :, None]
    skipped = skip_heads[None, None, :, None] * x_wide
    return (within + across + skipped).reshape(length, nheads * hwidth)

def reference(ssm_input, b_input, c_input, dt_input, conv_weight, conv_bias, a_log, dt_bias, skip_gain, grad_out):
    per_dev = H // N_SP
    group_devs = N_SP // G
    length = ssm_input.shape[1]
    outputs = []
    kernel_total = jnp.zeros(conv_weight.shape, jnp.float32)
    offset_total = jnp.zeros(conv_bias.shape, jnp.float32)
    head_total = jnp.zeros((3, H), jnp.float32)
    for seq_index in range(SEQS):
        x_full = jnp.concatenate([jnp.zeros((K - 1, H * P_SIZE), jnp.float32), ssm_input[seq_index].astype(jnp.float32)], 0)
        b_full = jnp.concatenate([jnp.zeros((K - 1, G * N), jnp.float32), b_input[seq_index].astype(jnp.float32)], 0)
        c_full = jnp.concatenate([jnp.zeros((K - 1, G * N), jnp.float32), c_input[seq_index].astype(jnp.float32)], 0)
        conv_outs, conv_back = jax.vjp(conv_all, x_full, b_full, c_full, conv_weight, conv_bias)
        x_conv = conv_outs[0].astype(jnp.bfloat16)
        b_conv = conv_outs[1].astype(jnp.bfloat16)
        c_conv = conv_outs[2].astype(jnp.bfloat16)
        dt_rows = dt_input[seq_index]
        dy_rows = grad_out[seq_index]

        def one_set(set_index):
            first_col = (set_index * per_dev * P_SIZE).astype(jnp.int32)
            first_head = (set_index * per_dev).astype(jnp.int32)
            group_col = (set_index // group_devs * N).astype(jnp.int32)
            x_heads = lax.dynamic_slice_in_dim(x_conv, first_col, per_dev * P_SIZE, 1)
            dy_heads = lax.dynamic_slice_in_dim(dy_rows, first_col, per_dev * P_SIZE, 1)
            dt_heads = lax.dynamic_slice_in_dim(dt_rows, first_head, per_dev, 1)
            b_group = lax.dynamic_slice_in_dim(b_conv, group_col, N, 1)
            c_group = lax.dynamic_slice_in_dim(c_conv, group_col, N, 1)
            alog_heads = lax.dynamic_slice_in_dim(a_log, first_head, per_dev)
            dtbias_heads = lax.dynamic_slice_in_dim(dt_bias, first_head, per_dev)
            skip_heads = lax.dynamic_slice_in_dim(skip_gain, first_head, per_dev)
            y_heads, ssd_back = jax.vjp(ssd_block, x_heads, dt_heads, b_group, c_group, alog_heads, dtbias_heads, skip_heads)
            grads = ssd_back(dy_heads.astype(jnp.float32))
            return (y_heads.astype(jnp.bfloat16),) + tuple(grads)
        results = lax.map(one_set, jnp.arange(N_SP, dtype=jnp.int32))
        y_rows = jnp.transpose(results[0], (1, 0, 2)).reshape(length, H * P_SIZE)
        gx_rows = jnp.transpose(results[1], (1, 0, 2)).reshape(length, H * P_SIZE)
        gdt_rows = jnp.transpose(results[2], (1, 0, 2)).reshape(length, H)
        gb_sum = results[3].astype(jnp.float32).reshape(G, group_devs, length, N).sum(axis=1)
        gc_sum = results[4].astype(jnp.float32).reshape(G, group_devs, length, N).sum(axis=1)
        gb_sum = jnp.transpose(gb_sum, (1, 0, 2)).reshape(length, G * N)
        gc_sum = jnp.transpose(gc_sum, (1, 0, 2)).reshape(length, G * N)
        head_terms = jnp.stack([results[5].reshape(H), results[6].reshape(H), results[7].reshape(H)])
        d_xfull, d_bfull, d_cfull, d_kernel, d_offset = conv_back((gx_rows.astype(jnp.float32), gb_sum, gc_sum))
        kernel_total = kernel_total + d_kernel
        offset_total = offset_total + d_offset
        head_total = head_total + head_terms
        outputs.append((y_rows, d_xfull[K - 1:].astype(jnp.bfloat16), d_bfull[K - 1:].astype(jnp.bfloat16), d_cfull[K - 1:].astype(jnp.bfloat16), gdt_rows))
    y_out = jnp.stack([entry[0] for entry in outputs])
    grad_x = jnp.stack([entry[1] for entry in outputs])
    grad_b = jnp.stack([entry[2] for entry in outputs])
    grad_c = jnp.stack([entry[3] for entry in outputs])
    grad_dt = jnp.stack([entry[4] for entry in outputs])
    return (y_out, grad_x, grad_b, grad_c, grad_dt, kernel_total, offset_total, head_total)
```

```python
import functools

import jax
import jax.numpy as jnp
from jax import lax
from jax.experimental import pallas as pl
from jax.experimental.pallas import tpu as pltpu
from jax.sharding import PartitionSpec as P

MESH = pl.DeviceIdType.MESH
F32 = jnp.float32
BF = jnp.bfloat16
N = 256
Q = 128
NY = 4
NB = 4
T = NB * Q
NSEG = 16
XW = 2048
CW = 256
NCH = XW // CW
HALO = 16
NPIECE = 32
HP = lax.Precision.HIGHEST
ANY = pl.BlockSpec(memory_space=pl.ANY)
VM = pl.BlockSpec(memory_space=pltpu.VMEM)
VLIM = 60 * 1024 * 1024


def dot(a, b, ca, cb):
    return lax.dot_general(a, b, (((ca,), (cb,)), ((), ())), preferred_element_type=F32)


def remote(src, dst, send, recv, target):
    return pltpu.make_async_remote_copy(
        src_ref=src, dst_ref=dst, send_sem=send, recv_sem=recv,
        device_id={"sp": target}, device_id_type=MESH,
    )


def place():
    me = lax.axis_index("sp")
    return me, lax.rem(me, NY), lax.div(me, NY)


def greet(targets, extra=None):
    barrier = pltpu.get_barrier_semaphore()
    for t in targets:
        pl.semaphore_signal(barrier, inc=1, device_id={"sp": t}, device_id_type=MESH)
    return barrier


def bring_kernel(x, dy, b, c, dt, xo, dyo, bo, co, dto, xh, bh, ch, stage, stage_s, send, recv, hs, hr, loc):
    me, y, seg = place()
    base = seg * NY
    nxt = lax.rem(seg + 1, NSEG) * NY
    prv = lax.rem(seg + NSEG - 1, NSEG) * NY + NY - 1
    peers = [base + lax.rem(y + i, NY) for i in (1, 3, 2)]
    barrier = greet(peers + [prv])

    @pl.when(y == NY - 1)
    def _():
        for j in range(NY):
            pl.semaphore_signal(barrier, inc=1, device_id={"sp": nxt + j}, device_id_type=MESH)

    pl.semaphore_wait(barrier, jnp.where(y == NY - 1, 2 * NY, NY))
    rows = pl.ds(pl.multiple_of(y * Q, Q), Q)

    def cols(j, w):
        return pl.ds(pl.multiple_of(j * w, w), w)

    arrays = ((x, xo, XW), (dy, dyo, XW), (b, bo, N), (c, co, N))

    @pl.when(y == NY - 1)
    def _():
        for j in range(NY):
            for n, (src, dst, w) in enumerate(((x, xh, XW), (b, bh, N), (c, ch, N))):
                remote(src.at[pl.ds(Q - HALO, HALO), pl.ds(j * w, w)], dst, hs.at[j, n], hr.at[n], nxt + j).start()

    copies = []
    for n, (src, dst, w) in enumerate(arrays):
        for i, k in enumerate((1, 3, 2)):
            j = lax.rem(y + k, NY)
            cp = remote(src.at[:, cols(j, w)], dst.at[rows, :], send.at[n, i], recv.at[n, i], peers[i])
            cp.start()
            copies.append(cp)
    for i in range(3):
        cp = remote(dt, dto.at[rows, :], send.at[4, i], recv.at[4, i], peers[i])
        cp.start()
        copies.append(cp)
    ins = []
    for n, (src, dst, w) in enumerate(arrays):
        st = stage.at[n] if w == XW else stage_s.at[n - 2]
        cp = pltpu.make_async_copy(src.at[:, cols(y, w)], st, loc.at[n])
        cp.start()
        ins.append((cp, st, dst))
    dst_stage = stage_s.at[2, :, pl.ds(0, 128)]
    cp = pltpu.make_async_copy(dt, dst_stage, loc.at[4])
    cp.start()
    ins.append((cp, dst_stage, dto))
    outs = []
    for n, (cp, st, dst) in enumerate(ins):
        cp.wait()
        o = pltpu.make_async_copy(st, dst.at[rows, :], loc.at[5 + n])
        o.start()
        outs.append(o)
    for o in outs:
        o.wait()
    for n, (src, dst, w) in enumerate(((x, xh, XW), (b, bh, N), (c, ch, N))):
        remote(src.at[pl.ds(Q - HALO, HALO), pl.ds(0, w)], dst, hs.at[0, n], hr.at[n], prv).wait_recv()
    for cp in copies:
        cp.wait_recv()
    for cp in copies:
        cp.wait_send()

    @pl.when(y == NY - 1)
    def _():
        for j in range(NY):
            for n, (src, dst, w) in enumerate(((x, xh, XW), (b, bh, N), (c, ch, N))):
                remote(src.at[pl.ds(Q - HALO, HALO), pl.ds(j * w, w)], dst, hs.at[j, n], hr.at[n], nxt + j).wait_send()


def bring(x, dy, b, c, dt):
    s = jax.ShapeDtypeStruct
    return pl.pallas_call(
        bring_kernel,
        name="tokens_to_heads",
        out_shape=(s((T, XW), BF), s((T, XW), BF), s((T, N), BF), s((T, N), BF), s((T, 128), BF),
                   s((HALO, XW), BF), s((HALO, N), BF), s((HALO, N), BF)),
        in_specs=[ANY] * 5,
        out_specs=[ANY] * 8,
        scratch_shapes=[
            pltpu.VMEM((2, Q, XW), BF),
            pltpu.VMEM((3, Q, N), BF),
            pltpu.SemaphoreType.DMA((5, 3)),
            pltpu.SemaphoreType.DMA((5, 3)),
            pltpu.SemaphoreType.DMA((4, 3)),
            pltpu.SemaphoreType.DMA((3,)),
            pltpu.SemaphoreType.DMA((10,)),
        ],
        compiler_params=pltpu.CompilerParams(collective_id=0, has_side_effects=True),
    )(x, dy, b, c, dt)


def spread(cols):
    lane = lax.broadcasted_iota(jnp.int32, (cols.shape[0], 128), 1) < 64
    parts = [jnp.where(lane, cols[:, h : h + 1], cols[:, h + 1 : h + 2]) for h in range(0, CW // 64, 2)]
    return jnp.concatenate(parts, axis=1)


def fill(pad, halo, raw):
    pad[0:8, :] = halo[HALO - 8 :, :].astype(F32)
    pad[8 : 8 + T, :] = raw[...].astype(F32)


def conv_rows(pad, w, bias, k):
    total = bias
    for j in range(4):
        total = total + w[j : j + 1, :] * pad[5 + j + k * Q : 5 + j + k * Q + Q, :]
    return total


def sigmoid(s):
    return 1.0 / (1.0 + jnp.exp(-s))


def local_kernel(x, xh, dy, w, bias, b, bh, c, ch, wb, wc, rs,
                 bo, co, bto, cto, so, do, pad):
    @pl.when(pl.program_id(0) == 0)
    def _():
        for raw, halo, wt, out, outt in ((b, bh, wb, bo, bto), (c, ch, wc, co, cto)):
            fill(pad, halo, raw)
            for k in range(NB):
                s = conv_rows(pad, wt[...], wt[4:5, :], k)
                v = (s * sigmoid(s)).astype(BF)
                out[k * Q : (k + 1) * Q, :] = v
                outt[:, k * Q : (k + 1) * Q] = jnp.transpose(v)

    fill(pad, xh, x)
    wx = w[...]
    S = jnp.zeros((N, CW), F32)
    for k in range(NB):
        sl = slice(k * Q, (k + 1) * Q)
        s = conv_rows(pad, wx, wx[4:5, :], k)
        xc = (s * sigmoid(s)).astype(BF).astype(F32)
        r = spread(rs[0, sl, 0:4])
        st = spread(rs[0, sl, 4:8])
        re = r[Q - 1 : Q, :]
        wt = (xc * (st * jnp.exp(re - r))).astype(BF)
        S = jnp.exp(re) * S + dot(bto[:, sl], wt, 1, 0)
    D = jnp.zeros((N, CW), F32)
    for k in reversed(range(NB)):
        sl = slice(k * Q, (k + 1) * Q)
        r = spread(rs[0, sl, 0:4])
        re = r[Q - 1 : Q, :]
        v = (dy[sl, :].astype(F32) * jnp.exp(r)).astype(BF)
        D = jnp.exp(re) * D + dot(cto[:, sl], v, 1, 0)
    for i in range(2):
        for j in range(2):
            so[2 * i + j] = S[i * 128 : (i + 1) * 128, j * 128 : (j + 1) * 128]
            do[2 * i + j] = D[i * 128 : (i + 1) * 128, j * 128 : (j + 1) * 128]


def chunked(rows):
    return pl.BlockSpec((rows, CW), lambda i: (0, i))


def whole(*shape):
    return pl.BlockSpec(shape, lambda i: (0,) * len(shape))


PIECES = pl.BlockSpec((4, 128, 128), lambda i: (i, 0, 0))
RS = pl.BlockSpec((1, T, 8), lambda i: (i, 0, 0))
RT = pl.BlockSpec((1, 8, T), lambda i: (i, 0, 0))


def local_states(x, xh, dy, w, b, bh, c, ch, wb, wc, rs):
    s = jax.ShapeDtypeStruct

    def kern(x, xh, dy, w, b, bh, c, ch, wb, wc, rs, *rest):
        local_kernel(x, xh, dy, w, None, b, bh, c, ch, wb, wc, rs, *rest)

    return pl.pallas_call(
        kern,
        name="local_states",
        grid=(NCH,),
        out_shape=(s((T, N), BF), s((T, N), BF), s((N, T), BF), s((N, T), BF),
                   s((NPIECE, 128, 128), F32), s((NPIECE, 128, 128), F32)),
        in_specs=[chunked(T), chunked(HALO), chunked(T), chunked(8), whole(T, N), whole(HALO, N),
                  whole(T, N), whole(HALO, N), whole(8, N), whole(8, N), RS],
        out_specs=[whole(T, N), whole(T, N), whole(N, T), whole(N, T), PIECES, PIECES],
        scratch_shapes=[pltpu.VMEM((T + 8, CW), F32)],
        compiler_params=pltpu.CompilerParams(vmem_limit_bytes=VLIM),
    )(x, xh, dy, w, b, bh, c, ch, wb, wc, rs)


STEP = 3


def chain_kernel(sl, dl, decay, so, do, sbuf, dbuf, ss, sr, ds, dr):
    me, y, seg = place()
    up = lax.rem(seg + 1, NSEG) * NY + y
    down = lax.rem(seg + NSEG - 1, NSEG) * NY + y
    barrier = greet([up, down])
    pl.semaphore_wait(barrier, 2)

    def half(index, first, last, loc, out, buf, send, recv, target, source):
        @pl.when((index >= 0) & (index < NPIECE))
        def _():
            @pl.when(jnp.logical_not(first))
            def _():
                remote(buf.at[index], out.at[index], send.at[index], recv.at[index], source).wait_recv()

            @pl.when(first)
            def _():
                out[index] = jnp.zeros((128, 128), BF)

            @pl.when(jnp.logical_not(last))
            def _():
                buf[index] = (out[index].astype(F32) * decay[index, 0:1, :] + loc[index]).astype(BF)
                remote(buf.at[index], out.at[index], send.at[index], recv.at[index], target).start()

    def step(n, carry):
        half(n - STEP * seg, seg == 0, seg == NSEG - 1, sl, so, sbuf, ss, sr, up, down)
        half(n - STEP * (NSEG - 1 - seg), seg == NSEG - 1, seg == 0, dl, do, dbuf, ds, dr, down, up)
        return carry

    lax.fori_loop(0, NPIECE + STEP * (NSEG - 1), step, 0)

    def drain(n, carry):
        @pl.when(seg != NSEG - 1)
        def _():
            remote(sbuf.at[n], so.at[n], ss.at[n], sr.at[n], up).wait_send()

        @pl.when(seg != 0)
        def _():
            remote(dbuf.at[n], do.at[n], ds.at[n], dr.at[n], down).wait_send()

        return carry

    lax.fori_loop(0, NPIECE, drain, 0)


def chains(sl, dl, decay):
    s = jax.ShapeDtypeStruct((NPIECE, 128, 128), BF)
    return pl.pallas_call(
        chain_kernel,
        name="state_chains",
        out_shape=(s, s),
        in_specs=[VM] * 3,
        out_specs=[VM] * 2,
        scratch_shapes=[
            pltpu.VMEM((NPIECE, 128, 128), BF),
            pltpu.VMEM((NPIECE, 128, 128), BF),
        ] + [pltpu.SemaphoreType.DMA((NPIECE,))] * 4,
        compiler_params=pltpu.CompilerParams(collective_id=1, has_side_effects=True, vmem_limit_bytes=VLIM),
    )(sl, dl, decay)


def join(ref):
    return jnp.concatenate(
        [jnp.concatenate([ref[2 * i], ref[2 * i + 1]], axis=1) for i in range(2)], axis=0
    ).astype(F32)


def conv_back(pad, dpad, w, out, last, corr, dw):
    dpad[T : T + 8, :] = jnp.zeros((8, pad.shape[1]), F32)
    sums = [jnp.zeros((1, pad.shape[1]), F32) for _ in range(5)]
    for k in range(NB):
        d0 = dpad[k * Q : (k + 1) * Q, :]
        for j in range(4):
            sums[j] = sums[j] + jnp.sum(d0 * pad[5 + j + k * Q : 5 + j + k * Q + Q, :], axis=0, keepdims=True)
        sums[4] = sums[4] + jnp.sum(d0, axis=0, keepdims=True)
        g = w[3:4, :] * d0
        for j in range(3):
            g = g + w[j : j + 1, :] * dpad[3 - j + k * Q : 3 - j + (k + 1) * Q, :]
        out[k * Q : (k + 1) * Q, :] = g.astype(BF)
        if k == NB - 1:
            last[...] = g[Q - 16 :, :]
    z = jnp.zeros((1, pad.shape[1]), F32)
    d = [dpad[m : m + 1, :] for m in range(3)]
    ws = [w[j : j + 1, :] for j in range(3)]
    corr[...] = jnp.concatenate(
        [z] * 5 + [ws[0] * d[0], ws[1] * d[0] + ws[0] * d[1], ws[2] * d[0] + ws[1] * d[1] + ws[0] * d[2]], axis=0
    )
    dw[...] = jnp.concatenate(sums + [z] * 3, axis=0)


def final_kernel(x, xh, dy, w, b, bh, c, ch, wb, wc, rs, rt, skip, bc, cc, bct, cct, sin, din,
                 yo, gxo, xlast, xcorr, xdw, gbo, blast, bcorr, bdw, gco, clast, ccorr, cdw, qo, dso,
                 pad, dpad, S, sc, gacc, db, dc):
    pid = pl.program_id(0)

    @pl.when(pid == 0)
    def _():
        for k in range(NB):
            sl = slice(k * Q, (k + 1) * Q)
            sc[k] = dot(cc[sl, :], bc[sl, :], 1, 1)
        gacc[...] = jnp.zeros_like(gacc)
        db[...] = jnp.zeros_like(db)
        dc[...] = jnp.zeros_like(dc)
        qo[...] = jnp.zeros_like(qo)

    fill(pad, xh, x)
    wx = w[...]
    S[0] = join(sin)
    for k in range(NB):
        sl = slice(k * Q, (k + 1) * Q)
        s = conv_rows(pad, wx, wx[4:5, :], k)
        xc = (s * sigmoid(s)).astype(BF).astype(F32)
        r = spread(rs[0, sl, 0:4])
        st = spread(rs[0, sl, 4:8])
        re = r[Q - 1 : Q, :]
        wt = (xc * (st * jnp.exp(re - r))).astype(BF)
        S[k + 1] = jnp.exp(re) * S[k] + dot(bct[:, sl], wt, 1, 0)

    D = join(din)
    causal = lax.broadcasted_iota(jnp.int32, (Q, Q), 0) >= lax.broadcasted_iota(jnp.int32, (Q, Q), 1)
    low = lax.broadcasted_iota(jnp.int32, (Q, 128), 1) < 64
    er = lax.broadcasted_iota(jnp.int32, (CW, 128), 0) // 64 + pid * (CW // 64)
    el = lax.broadcasted_iota(jnp.int32, (CW, 128), 1)
    ends = []
    for k in reversed(range(NB)):
        sl = slice(k * Q, (k + 1) * Q)
        s = conv_rows(pad, wx, wx[4:5, :], k)
        sg = sigmoid(s)
        xcb = (s * sg).astype(BF)
        xc = xcb.astype(F32)
        dyb = dy[sl, :]
        dyf = dyb.astype(F32)
        rc = rs[0, sl, 0:4]
        r = spread(rc)
        st = spread(rs[0, sl, 4:8])
        re = r[Q - 1 : Q, :]
        er_ = jnp.exp(r)
        ee = jnp.exp(re - r)
        ub = (xc * st).astype(BF)
        wt = (xc * (st * ee)).astype(BF)
        v = (dyf * er_).astype(BF)
        Sb = S[k].astype(BF)
        Db = D.astype(BF)
        ends.append(jnp.sum(D * S[k + 1], axis=0, keepdims=True))
        ya = er_ * dot(cc[sl, :], Sb, 1, 0)
        du = ee * dot(bc[sl, :], Db, 1, 0)
        db[sl, :] += dot(wt, Db, 1, 1)
        dc[sl, :] += dot(v, Sb, 1, 1)
        yw, dw_ = [], []
        g = sc[k]
        acc = gacc[k]
        zero = jnp.zeros((Q, 128), BF)
        for p in range(CW // 128):
            ls = []
            for h in (2 * p, 2 * p + 1):
                gap = rc[:, h : h + 1] - rt[0, h : h + 1, sl]
                ls.append(jnp.exp(jnp.where(causal, gap, -1e30)))
            up = ub[:, p * 128 : (p + 1) * 128]
            dp = dyb[:, p * 128 : (p + 1) * 128]
            ublk = jnp.concatenate([jnp.where(low, up, zero), jnp.where(low, zero, up)], axis=0)
            dblk = jnp.concatenate([jnp.where(low, dp, zero), jnp.where(low, zero, dp)], axis=0)
            ms = [(g * l).astype(BF) for l in ls]
            yw.append(dot(jnp.concatenate(ms, axis=1), ublk, 1, 0))
            dw_.append(dot(jnp.concatenate(ms, axis=0), dblk, 0, 0))
            dm = dot(dp, ublk, 1, 1)
            acc = acc + dm[:, :Q] * ls[0] + dm[:, Q:] * ls[1]
        gacc[k] = acc
        yin = ya + jnp.concatenate(yw, axis=1)
        du = du + jnp.concatenate(dw_, axis=1)
        sk = skip[0:1, :]
        yo[sl, :] = (yin + sk * xc).astype(BF)
        qs = (dyf * yin - ub.astype(F32) * du, xc * du, dyf * xc)
        total = jnp.zeros((Q, 128), F32)
        for i, q in enumerate(qs):
            e = (el == er + 32 * i).astype(BF)
            hi = q.astype(BF)
            lo = (q - hi.astype(F32)).astype(BF)
            total = total + dot(hi, e, 1, 0) + dot(lo, e, 1, 0)
        qo[sl, :] += total
        gx = st * du + sk * dyf
        dpad[sl, :] = gx * (sg * (1.0 + s * (1.0 - sg)))
        D = jnp.exp(re) * D + dot(cct[:, sl], v, 1, 0)
    dso[...] = jnp.concatenate(ends[::-1] + [jnp.zeros((4, CW), F32)], axis=0)
    conv_back(pad, dpad, wx, gxo, xlast, xcorr, xdw)

    @pl.when(pid == NCH - 1)
    def _():
        for raw, halo, wt, gout, lst, crr, dwo, acc, other, tr in (
            (b, bh, wb, gbo, blast, bcorr, bdw, db, cc, True),
            (c, ch, wc, gco, clast, ccorr, cdw, dc, bc, False),
        ):
            fill(pad, halo, raw)
            for k in range(NB):
                sl = slice(k * Q, (k + 1) * Q)
                gk = gacc[k].astype(BF)
                tot = acc[sl, :] + dot(gk, other[sl, :], 0 if tr else 1, 0)
                s = conv_rows(pad, wt[...], wt[4:5, :], k)
                sg = sigmoid(s)
                dpad[sl, :] = tot * (sg * (1.0 + s * (1.0 - sg)))
            conv_back(pad, dpad, wt[...], gout, lst, crr, dwo)


def finals(x, xh, dy, w, b, bh, c, ch, wb, wc, rs, rt, skip, bc, cc, bct, cct, sin, din):
    s = jax.ShapeDtypeStruct
    bx = [whole(T, N), whole(16, N), whole(8, N), whole(8, N)]
    bs = [s((T, N), BF), s((16, N), F32), s((8, N), F32), s((8, N), F32)]
    return pl.pallas_call(
        final_kernel,
        name="outputs_and_gradients",
        grid=(NCH,),
        out_shape=[s((T, XW), BF), s((T, XW), BF), s((16, XW), F32), s((8, XW), F32), s((8, XW), F32)]
        + bs + bs + [s((T, 128), F32), s((8, XW), F32)],
        in_specs=[chunked(T), chunked(HALO), chunked(T), chunked(8), whole(T, N), whole(HALO, N),
                  whole(T, N), whole(HALO, N), whole(8, N), whole(8, N), RS, RT, chunked(8),
                  whole(T, N), whole(T, N), whole(N, T), whole(N, T), PIECES, PIECES],
        out_specs=[chunked(T), chunked(T), chunked(16), chunked(8), chunked(8)] + bx + bx
        + [whole(T, 128), chunked(8)],
        scratch_shapes=[
            pltpu.VMEM((T + 8, CW), F32),
            pltpu.VMEM((T + 8, CW), F32),
            pltpu.VMEM((NB + 1, N, CW), F32),
            pltpu.VMEM((NB, Q, Q), F32),
            pltpu.VMEM((NB, Q, Q), F32),
            pltpu.VMEM((T, N), F32),
            pltpu.VMEM((T, N), F32),
        ],
        compiler_params=pltpu.CompilerParams(vmem_limit_bytes=VLIM),
    )(x, xh, dy, w, b, bh, c, ch, wb, wc, rs, rt, skip, bc, cc, bct, cct, sin, din)


def give_kernel(yf, gx, gb, gc, gdt, lx, lb, lc, kx, kb, kc,
                yo, gxo, gbo, gco, gdo,
                stage, stage_s, hx, hb, hc, tx, tb, tc, dts, send, recv, ks, kr, ts, tr, loc):
    me, y, seg = place()
    base = seg * NY
    up = lax.rem(seg + 1, NSEG) * NY + y
    down = lax.rem(seg + NSEG - 1, NSEG) * NY + y
    peers = [base + lax.rem(y + i, NY) for i in (1, 3, 2)]
    barrier = greet(peers + [up, down])
    pl.semaphore_wait(barrier, 5)
    halos = [remote(src, dst, ks.at[n], kr.at[n], down) for n, (src, dst) in enumerate(((kx, hx), (kb, hb), (kc, hc)))]
    for cp in halos:
        cp.start()

    def cols(w):
        return pl.ds(pl.multiple_of(y * w, w), w)

    arrays = ((yf, yo, XW, Q), (gx, gxo, XW, Q - 16), (gb, gbo, N, Q - 16), (gc, gco, N, Q - 16))
    copies = []
    for n, (src, dst, w, rows) in enumerate(arrays):
        for i, k in enumerate((1, 3, 2)):
            j = lax.rem(y + k, NY)
            rs = pl.ds(pl.multiple_of(j * Q, Q), rows)
            cp = remote(src.at[rs, :], dst.at[pl.ds(0, rows), cols(w)], send.at[n, i], recv.at[n, i], peers[i])
            cp.start()
            copies.append(cp)
    for i, k in enumerate((1, 3, 2)):
        j = lax.rem(y + k, NY)
        rs = pl.ds(pl.multiple_of(j * Q, Q), Q)
        cp = remote(gdt.at[rs, :], dts.at[i], send.at[4, i], recv.at[4, i], peers[i])
        cp.start()
        copies.append(cp)
    mine = pl.ds(pl.multiple_of(y * Q, Q), Q)
    tails = ((gx, gxo, XW, tx), (gb, gbo, N, tb), (gc, gco, N, tc))
    for n, (cp, t, l, h) in enumerate(zip(halos, (tx, tb, tc), (lx, lb, lc), (hx, hb, hc))):
        cp.wait_recv()

        @pl.when(seg == NSEG - 1)
        def _():
            t[...] = l[...].astype(BF)

        @pl.when(seg != NSEG - 1)
        def _():
            t[0:8, :] = l[0:8, :].astype(BF)
            t[8:16, :] = (l[8:16, :] + h[...]).astype(BF)

    def tail(n, i, k, do):
        src, dst, w, t = tails[n]
        j = lax.rem(y + k, NY)
        place_to = dst.at[pl.ds(Q - 16, 16), cols(w)]

        @pl.when(j == NY - 1)
        def _():
            do(remote(t, place_to, ts.at[n, i], tr.at[n, i], peers[i]))

        @pl.when(j != NY - 1)
        def _():
            rs = pl.ds(pl.multiple_of(j * Q + Q - 16, 16), 16)
            do(remote(src.at[rs, :], place_to, ts.at[n, i], tr.at[n, i], peers[i]))

    for n in range(3):
        for i, k in enumerate((1, 3, 2)):
            tail(n, i, k, lambda cp: cp.start())
    ins = []
    for n, (src, dst, w, rows) in enumerate(arrays):
        st = stage.at[n] if w == XW else stage_s.at[n - 2]
        cp = pltpu.make_async_copy(src.at[mine, :], st, loc.at[n])
        cp.start()
        ins.append((cp, st, dst, w))
    outs = []
    for n, (cp, st, dst, w) in enumerate(ins):
        cp.wait()
        if n > 0:
            t = tails[n - 1][3]

            @pl.when(y == NY - 1)
            def _():
                st[Q - 16 :, :] = t[...]

        o = pltpu.make_async_copy(st, dst.at[:, cols(w)], loc.at[4 + n])
        o.start()
        outs.append(o)
    own = pltpu.make_async_copy(gdt.at[mine, :], dts.at[3], loc.at[8])
    own.start()
    own.wait()
    for cp in copies[12:]:
        cp.wait_recv()
    gdo[...] = (dts[0].astype(F32) + dts[1].astype(F32) + dts[2].astype(F32) + dts[3].astype(F32)).astype(BF)
    for o in outs:
        o.wait()
    for cp in copies[:12]:
        cp.wait_recv()
    for n in range(3):
        for i, k in enumerate((1, 3, 2)):
            tail(n, i, k, lambda cp: cp.wait())
    for cp in copies:
        cp.wait_send()
    for cp in halos:
        cp.wait_send()


def give(*args):
    s = jax.ShapeDtypeStruct
    return pl.pallas_call(
        give_kernel,
        name="heads_to_tokens",
        out_shape=(s((Q, NY * XW), BF), s((Q, NY * XW), BF), s((Q, NY * N), BF), s((Q, NY * N), BF), s((Q, 128), BF)),
        in_specs=[ANY] * 5 + [VM] * 6,
        out_specs=[ANY] * 4 + [VM],
        scratch_shapes=[
            pltpu.VMEM((2, Q, XW), BF),
            pltpu.VMEM((2, Q, N), BF),
            pltpu.VMEM((8, XW), F32), pltpu.VMEM((8, N), F32), pltpu.VMEM((8, N), F32),
            pltpu.VMEM((16, XW), BF), pltpu.VMEM((16, N), BF), pltpu.VMEM((16, N), BF),
            pltpu.VMEM((4, Q, 128), BF),
            pltpu.SemaphoreType.DMA((5, 3)),
            pltpu.SemaphoreType.DMA((5, 3)),
            pltpu.SemaphoreType.DMA((3,)),
            pltpu.SemaphoreType.DMA((3,)),
            pltpu.SemaphoreType.DMA((3, 3)),
            pltpu.SemaphoreType.DMA((3, 3)),
            pltpu.SemaphoreType.DMA((9,)),
        ],
        compiler_params=pltpu.CompilerParams(collective_id=2, has_side_effects=True),
    )(*args)


def total_kernel(v, out, ra, rb, part, mid, s1, r1, s2, r2, s3, r3):
    dp = lax.axis_index("dp")
    me, y, seg = place()
    xh = lax.div(seg, 8)
    z = lax.rem(seg, 8)

    def to(d, h, zz, yy):
        return {"dp": d, "sp": h * 32 + zz * 4 + yy}

    along_z = [to(dp, xh, lax.rem(z + i, 8), y) for i in range(1, 8)]
    pos = dp * 2 + xh
    along_x = []
    for i in range(1, 8):
        q = lax.rem(pos + i, 8)
        along_x.append(to(lax.div(q, 2), lax.rem(q, 2), z, y))
    pzy = z * 4 + y
    along_zy = []
    for i in range(1, 32):
        q = lax.rem(pzy + i, 32)
        along_zy.append({"dp": dp, "sp": xh * 32 + q})
    barrier = pltpu.get_barrier_semaphore()
    for t in along_x + along_zy:
        pl.semaphore_signal(barrier, inc=1, device_id=t, device_id_type=MESH)
    pl.semaphore_wait(barrier, 38)

    def send(src, dst, a, b, t):
        cp = pltpu.make_async_remote_copy(src_ref=src, dst_ref=dst, send_sem=a, recv_sem=b, device_id=t, device_id_type=MESH)
        cp.start()
        return cp

    def block(i):
        return pl.ds(pl.multiple_of(i * 16, 16), 16)

    first = [send(v.at[block(lax.rem(z + i + 1, 8)), :], ra.at[z], s1.at[i], r1.at[i], t) for i, t in enumerate(along_z)]
    ra[z] = v[block(z), :]
    for cp in first:
        cp.wait()
    tot = ra[0]
    for i in range(1, 8):
        tot = tot + ra[i]
    part[...] = tot
    rb[pos] = tot
    second = [send(part, rb.at[pos], s2.at[i], r2.at[i], t) for i, t in enumerate(along_x)]
    for cp in second:
        cp.wait()
    tot = rb[0]
    for i in range(1, 8):
        tot = tot + rb[i]
    mid[...] = tot
    out[y, block(z), :] = tot
    third = [send(mid, out.at[y, block(z), :], s3.at[i], r3.at[i], t) for i, t in enumerate(along_zy)]
    for cp in third:
        cp.wait()


def totals(v):
    return pl.pallas_call(
        total_kernel,
        name="small_sums",
        out_shape=jax.ShapeDtypeStruct((NY, 128, 128), F32),
        in_specs=[VM],
        out_specs=VM,
        scratch_shapes=[
            pltpu.VMEM((8, 16, 128), F32),
            pltpu.VMEM((8, 16, 128), F32),
            pltpu.VMEM((16, 128), F32),
            pltpu.VMEM((16, 128), F32),
            pltpu.SemaphoreType.DMA((7,)), pltpu.SemaphoreType.DMA((7,)),
            pltpu.SemaphoreType.DMA((7,)), pltpu.SemaphoreType.DMA((7,)),
            pltpu.SemaphoreType.DMA((31,)), pltpu.SemaphoreType.DMA((31,)),
        ],
        compiler_params=pltpu.CompilerParams(collective_id=3, has_side_effects=True),
    )(v)


def per_device(ssm_input, b_input, c_input, dt_input, conv_weight, conv_bias, a_log, dt_bias, skip_gain, grad_out):
    me = lax.axis_index("sp")
    y = lax.rem(me, NY)
    seg = lax.div(me, NY)
    x, dy, b, c, dt, xh, bh, ch = bring(ssm_input[0], grad_out[0], b_input[0], c_input[0], dt_input[0])
    first = seg == 0
    xh, bh, ch = [jnp.where(first, jnp.zeros_like(h), h) for h in (xh, bh, ch)]
    taps = jnp.concatenate([conv_weight, conv_bias[None], jnp.zeros((3, conv_weight.shape[1]), F32)], 0)
    w = lax.dynamic_slice_in_dim(taps, y * XW, XW, 1)
    wb = lax.dynamic_slice_in_dim(taps, NY * XW + y * N, N, 1)
    wc = lax.dynamic_slice_in_dim(taps, NY * (XW + N) + y * N, N, 1)
    heads = XW // 64

    def own(v):
        return lax.dynamic_slice_in_dim(v, y * heads, heads, 0)

    rate = jnp.exp(own(a_log))
    raw = lax.dynamic_slice_in_dim(dt, y * heads, heads, 1).astype(F32) + own(dt_bias)[None, :]
    step = jax.nn.softplus(raw)
    logs = -step * rate[None, :]
    tril = (jnp.arange(Q)[:, None] >= jnp.arange(Q)[None, :]).astype(F32)
    run = jnp.einsum("ts,ksh->kth", tril, logs.reshape(NB, Q, heads), precision=HP)
    whole_decay = jnp.exp(run[:, -1, :].sum(0))
    run = run.reshape(T, heads)
    per = CW // 64
    rs = jnp.concatenate([run.reshape(T, NCH, per), step.reshape(T, NCH, per)], 2).transpose(1, 0, 2)
    rt = jnp.pad(run.reshape(T, NCH, per).transpose(1, 2, 0), ((0, 0), (0, 8 - per), (0, 0)))
    skip = jnp.broadcast_to(jnp.repeat(own(skip_gain), 64)[None, :], (8, XW))
    lanes = jnp.repeat(whole_decay, 64).reshape(NCH, 1, 2, 128)
    decay = jnp.broadcast_to(lanes, (NCH, 2, 2, 128)).reshape(NPIECE, 1, 128)
    decay = jnp.broadcast_to(decay, (NPIECE, 8, 128))
    bc, cc, bct, cct, sl, dl = local_states(x, xh, dy, w, b, bh, c, ch, wb, wc, rs)
    sin, din = chains(sl, dl, decay)
    (yf, gx, xlast, xcorr, xdw, gb, blast, bcorr, bdw, gc, clast, ccorr, cdw, qs, ends) = finals(
        x, xh, dy, w, b, bh, c, ch, wb, wc, rs, rt, skip, bc, cc, bct, cct, sin, din
    )
    q1 = qs[:, :heads].reshape(NB, Q, heads)
    end = ends[:NB].reshape(NB, heads, 64).sum(-1)
    dlog = (jnp.einsum("ts,kth->ksh", tril, q1, precision=HP) + end[:, None, :]).reshape(T, heads)
    dstep = qs[:, heads : 2 * heads] - dlog * rate[None, :]
    draw = dstep * jax.nn.sigmoid(raw)
    gdt = jnp.zeros((T, 128), BF)
    gdt = lax.dynamic_update_slice_in_dim(gdt, draw.astype(BF), y * heads, 1)
    hg = jnp.stack([(dlog * logs).sum(0), draw.sum(0), qs[:, 2 * heads : 3 * heads].sum(0)])
    v = jnp.concatenate([xdw[:5], bdw[:5], cdw[:5]], 1).reshape(100, 128)
    hrow = jnp.pad(hg.reshape(1, 3 * heads), ((0, 27), (0, 128 - 3 * heads)))
    tot = totals(jnp.concatenate([v, hrow], 0))
    grads = tot[:, :100, :].reshape(NY, 5, XW + 2 * N).transpose(1, 0, 2)
    gw = jnp.concatenate(
        [grads[:, :, :XW].reshape(5, -1), grads[:, :, XW : XW + N].reshape(5, -1), grads[:, :, XW + N :].reshape(5, -1)], 1
    )
    hsum = tot[:, 100, : 3 * heads].reshape(NY, 3, heads).transpose(1, 0, 2).reshape(3, NY * heads)
    hsum = lax.dynamic_slice_in_dim(hsum, me * 2, 2, 1)
    yo, gxo, gbo, gco, gdo = give(yf, gx, gb, gc, gdt, xlast, blast, clast, xcorr, bcorr, ccorr)
    return (yo[None], gxo[None], gbo[None], gco[None], gdo[None], gw[:4], gw[4], hsum)


def solution(mesh):
    row = P("dp", "sp", None)
    return jax.shard_map(
        per_device, mesh=mesh,
        in_specs=(row, row, row, row, P(), P(), P(), P(), P(), row),
        out_specs=(row, row, row, row, row, P(), P(), P(None, "sp")),
        check_vma=False,
    )
```

```python
import functools

import jax
import jax.numpy as jnp
from jax import lax
from jax.experimental import pallas as pl
from jax.experimental.pallas import tpu as pltpu
from jax.sharding import PartitionSpec as P

MESH = pl.DeviceIdType.MESH
F32 = jnp.float32
BF = jnp.bfloat16
N = 256
Q = 128
NY = 4
NB = 4
T = NB * Q
NSEG = 16
XW = 2048
CW = 256
NCH = XW // CW
HALO = 16
NPIECE = 32
HP = lax.Precision.HIGHEST
ANY = pl.BlockSpec(memory_space=pl.ANY)
VM = pl.BlockSpec(memory_space=pltpu.VMEM)
VLIM = 60 * 1024 * 1024


def dot(a, b, ca, cb):
    return lax.dot_general(a, b, (((ca,), (cb,)), ((), ())), preferred_element_type=F32)


def remote(src, dst, send, recv, target):
    return pltpu.make_async_remote_copy(
        src_ref=src, dst_ref=dst, send_sem=send, recv_sem=recv,
        device_id={"sp": target}, device_id_type=MESH,
    )


def place():
    me = lax.axis_index("sp")
    return me, lax.rem(me, NY), lax.div(me, NY)


def greet(targets, extra=None):
    barrier = pltpu.get_barrier_semaphore()
    for t in targets:
        pl.semaphore_signal(barrier, inc=1, device_id={"sp": t}, device_id_type=MESH)
    return barrier


def bring_kernel(x, dy, b, c, dt, xo, dyo, bo, co, dto, xh, bh, ch, stage, stage_s, send, recv, hs, hr, loc):
    me, y, seg = place()
    base = seg * NY
    nxt = lax.rem(seg + 1, NSEG) * NY
    prv = lax.rem(seg + NSEG - 1, NSEG) * NY + NY - 1
    peers = [base + lax.rem(y + i, NY) for i in (1, 3, 2)]
    barrier = greet(peers + [prv])

    @pl.when(y == NY - 1)
    def _():
        for j in range(NY):
            pl.semaphore_signal(barrier, inc=1, device_id={"sp": nxt + j}, device_id_type=MESH)

    pl.semaphore_wait(barrier, jnp.where(y == NY - 1, 2 * NY, NY))
    rows = pl.ds(pl.multiple_of(y * Q, Q), Q)

    def cols(j, w):
        return pl.ds(pl.multiple_of(j * w, w), w)

    arrays = ((x, xo, XW), (dy, dyo, XW), (b, bo, N), (c, co, N))

    @pl.when(y == NY - 1)
    def _():
        for j in range(NY):
            for n, (src, dst, w) in enumerate(((x, xh, XW), (b, bh, N), (c, ch, N))):
                remote(src.at[pl.ds(Q - HALO, HALO), pl.ds(j * w, w)], dst, hs.at[j, n], hr.at[n], nxt + j).start()

    copies = []
    for n, (src, dst, w) in enumerate(arrays):
        for i, k in enumerate((1, 3, 2)):
            j = lax.rem(y + k, NY)
            cp = remote(src.at[:, cols(j, w)], dst.at[rows, :], send.at[n, i], recv.at[n, i], peers[i])
            cp.start()
            copies.append(cp)
    for i in range(3):
        cp = remote(dt, dto.at[rows, :], send.at[4, i], recv.at[4, i], peers[i])
        cp.start()
        copies.append(cp)
    ins = []
    for n, (src, dst, w) in enumerate(arrays):
        st = stage.at[n] if w == XW else stage_s.at[n - 2]
        cp = pltpu.make_async_copy(src.at[:, cols(y, w)], st, loc.at[n])
        cp.start()
        ins.append((cp, st, dst))
    dst_stage = stage_s.at[2, :, pl.ds(0, 128)]
    cp = pltpu.make_async_copy(dt, dst_stage, loc.at[4])
    cp.start()
    ins.append((cp, dst_stage, dto))
    outs = []
    for n, (cp, st, dst) in enumerate(ins):
        cp.wait()
        o = pltpu.make_async_copy(st, dst.at[rows, :], loc.at[5 + n])
        o.start()
        outs.append(o)
    for o in outs:
        o.wait()
    for n, (src, dst, w) in enumerate(((x, xh, XW), (b, bh, N), (c, ch, N))):
        remote(src.at[pl.ds(Q - HALO, HALO), pl.ds(0, w)], dst, hs.at[0, n], hr.at[n], prv).wait_recv()
    for cp in copies:
        cp.wait_recv()
    for cp in copies:
        cp.wait_send()

    @pl.when(y == NY - 1)
    def _():
        for j in range(NY):
            for n, (src, dst, w) in enumerate(((x, xh, XW), (b, bh, N), (c, ch, N))):
                remote(src.at[pl.ds(Q - HALO, HALO), pl.ds(j * w, w)], dst, hs.at[j, n], hr.at[n], nxt + j).wait_send()


def bring(x, dy, b, c, dt):
    s = jax.ShapeDtypeStruct
    return pl.pallas_call(
        bring_kernel,
        name="tokens_to_heads",
        out_shape=(s((T, XW), BF), s((T, XW), BF), s((T, N), BF), s((T, N), BF), s((T, 128), BF),
                   s((HALO, XW), BF), s((HALO, N), BF), s((HALO, N), BF)),
        in_specs=[ANY] * 5,
        out_specs=[ANY] * 8,
        scratch_shapes=[
            pltpu.VMEM((2, Q, XW), BF),
            pltpu.VMEM((3, Q, N), BF),
            pltpu.SemaphoreType.DMA((5, 3)),
            pltpu.SemaphoreType.DMA((5, 3)),
            pltpu.SemaphoreType.DMA((4, 3)),
            pltpu.SemaphoreType.DMA((3,)),
            pltpu.SemaphoreType.DMA((10,)),
        ],
        compiler_params=pltpu.CompilerParams(collective_id=0, has_side_effects=True),
    )(x, dy, b, c, dt)


def spread(cols):
    lane = lax.broadcasted_iota(jnp.int32, (cols.shape[0], 128), 1) < 64
    parts = [jnp.where(lane, cols[:, h : h + 1], cols[:, h + 1 : h + 2]) for h in range(0, CW // 64, 2)]
    return jnp.concatenate(parts, axis=1)


def fill(pad, halo, raw):
    pad[0:8, :] = halo[HALO - 8 :, :].astype(F32)
    pad[8 : 8 + T, :] = raw[...].astype(F32)


def conv_rows(pad, w, bias, k):
    total = bias
    for j in range(4):
        total = total + w[j : j + 1, :] * pad[5 + j + k * Q : 5 + j + k * Q + Q, :]
    return total


def sigmoid(s):
    return 1.0 / (1.0 + jnp.exp(-s))


def local_kernel(x, xh, dy, w, bias, b, bh, c, ch, wb, wc, rs,
                 bo, co, bto, cto, so, do, pad):
    @pl.when(pl.program_id(0) == 0)
    def _():
        for raw, halo, wt, out, outt in ((b, bh, wb, bo, bto), (c, ch, wc, co, cto)):
            fill(pad, halo, raw)
            for k in range(NB):
                s = conv_rows(pad, wt[...], wt[4:5, :], k)
                v = (s * sigmoid(s)).astype(BF)
                out[k * Q : (k + 1) * Q, :] = v
                outt[:, k * Q : (k + 1) * Q] = jnp.transpose(v)

    fill(pad, xh, x)
    wx = w[...]
    S = jnp.zeros((N, CW), F32)
    for k in range(NB):
        sl = slice(k * Q, (k + 1) * Q)
        s = conv_rows(pad, wx, wx[4:5, :], k)
        xc = (s * sigmoid(s)).astype(BF).astype(F32)
        r = spread(rs[0, sl, 0:4])
        st = spread(rs[0, sl, 4:8])
        re = r[Q - 1 : Q, :]
        wt = (xc * (st * jnp.exp(re - r))).astype(BF)
        S = jnp.exp(re) * S + dot(bto[:, sl], wt, 1, 0)
    D = jnp.zeros((N, CW), F32)
    for k in reversed(range(NB)):
        sl = slice(k * Q, (k + 1) * Q)
        r = spread(rs[0, sl, 0:4])
        re = r[Q - 1 : Q, :]
        v = (dy[sl, :].astype(F32) * jnp.exp(r)).astype(BF)
        D = jnp.exp(re) * D + dot(cto[:, sl], v, 1, 0)
    for i in range(2):
        for j in range(2):
            so[2 * i + j] = S[i * 128 : (i + 1) * 128, j * 128 : (j + 1) * 128]
            do[2 * i + j] = D[i * 128 : (i + 1) * 128, j * 128 : (j + 1) * 128]


def chunked(rows):
    return pl.BlockSpec((rows, CW), lambda i: (0, i))


def whole(*shape):
    return pl.BlockSpec(shape, lambda i: (0,) * len(shape))


PIECES = pl.BlockSpec((4, 128, 128), lambda i: (i, 0, 0))
RS = pl.BlockSpec((1, T, 8), lambda i: (i, 0, 0))
RT = pl.BlockSpec((1, 8, T), lambda i: (i, 0, 0))


def local_states(x, xh, dy, w, b, bh, c, ch, wb, wc, rs):
    s = jax.ShapeDtypeStruct

    def kern(x, xh, dy, w, b, bh, c, ch, wb, wc, rs, *rest):
        local_kernel(x, xh, dy, w, None, b, bh, c, ch, wb, wc, rs, *rest)

    return pl.pallas_call(
        kern,
        name="local_states",
        grid=(NCH,),
        out_shape=(s((T, N), BF), s((T, N), BF), s((N, T), BF), s((N, T), BF),
                   s((NPIECE, 128, 128), F32), s((NPIECE, 128, 128), F32)),
        in_specs=[chunked(T), chunked(HALO), chunked(T), chunked(8), whole(T, N), whole(HALO, N),
                  whole(T, N), whole(HALO, N), whole(8, N), whole(8, N), RS],
        out_specs=[whole(T, N), whole(T, N), whole(N, T), whole(N, T), PIECES, PIECES],
        scratch_shapes=[pltpu.VMEM((T + 8, CW), F32)],
        compiler_params=pltpu.CompilerParams(vmem_limit_bytes=VLIM),
    )(x, xh, dy, w, b, bh, c, ch, wb, wc, rs)


STEP = 5


def chain_kernel(sl, dl, decay, so, do, sbuf, dbuf, ss, sr, ds, dr):
    me, y, seg = place()
    up = lax.rem(seg + 1, NSEG) * NY + y
    down = lax.rem(seg + NSEG - 1, NSEG) * NY + y
    barrier = greet([up, down])
    pl.semaphore_wait(barrier, 2)

    def half(index, first, last, loc, out, buf, send, recv, target, source):
        @pl.when((index >= 0) & (index < NPIECE))
        def _():
            @pl.when(jnp.logical_not(first))
            def _():
                remote(buf.at[index], out.at[index], send.at[index], recv.at[index], source).wait_recv()

            @pl.when(first)
            def _():
                out[index] = jnp.zeros((128, 128), BF)

            @pl.when(jnp.logical_not(last))
            def _():
                buf[index] = (out[index].astype(F32) * decay[index, 0:1, :] + loc[index]).astype(BF)
                remote(buf.at[index], out.at[index], send.at[index], recv.at[index], target).start()

    def step(n, carry):
        half(n - STEP * seg, seg == 0, seg == NSEG - 1, sl, so, sbuf, ss, sr, up, down)
        half(n - STEP * (NSEG - 1 - seg), seg == NSEG - 1, seg == 0, dl, do, dbuf, ds, dr, down, up)
        return carry

    lax.fori_loop(0, NPIECE + STEP * (NSEG - 1), step, 0)

    def drain(n, carry):
        @pl.when(seg != NSEG - 1)
        def _():
            remote(sbuf.at[n], so.at[n], ss.at[n], sr.at[n], up).wait_send()

        @pl.when(seg != 0)
        def _():
            remote(dbuf.at[n], do.at[n], ds.at[n], dr.at[n], down).wait_send()

        return carry

    lax.fori_loop(0, NPIECE, drain, 0)


def chains(sl, dl, decay):
    s = jax.ShapeDtypeStruct((NPIECE, 128, 128), BF)
    return pl.pallas_call(
        chain_kernel,
        name="state_chains",
        out_shape=(s, s),
        in_specs=[VM] * 3,
        out_specs=[VM] * 2,
        scratch_shapes=[
            pltpu.VMEM((NPIECE, 128, 128), BF),
            pltpu.VMEM((NPIECE, 128, 128), BF),
        ] + [pltpu.SemaphoreType.DMA((NPIECE,))] * 4,
        compiler_params=pltpu.CompilerParams(collective_id=1, has_side_effects=True, vmem_limit_bytes=VLIM),
    )(sl, dl, decay)


WW = XW + 2 * N
VW = 3072
ZW = VW // 8


def join(ref):
    return jnp.concatenate(
        [jnp.concatenate([ref[2 * i], ref[2 * i + 1]], axis=1) for i in range(2)], axis=0
    ).astype(F32)


def pieces(q, count):
    out = []
    for _ in range(count):
        hi = q.astype(BF)
        out.append(hi)
        q = q - hi.astype(F32)
    return out


def conv_back(pad, dpad, w, out, last, corr, dw):
    dpad[T : T + 8, :] = jnp.zeros((8, pad.shape[1]), F32)
    sums = [jnp.zeros((1, pad.shape[1]), F32) for _ in range(5)]
    for k in range(NB):
        d0 = dpad[k * Q : (k + 1) * Q, :]
        for j in range(4):
            sums[j] = sums[j] + jnp.sum(d0 * pad[5 + j + k * Q : 5 + j + k * Q + Q, :], axis=0, keepdims=True)
        sums[4] = sums[4] + jnp.sum(d0, axis=0, keepdims=True)
        g = w[3:4, :] * d0
        for j in range(3):
            g = g + w[j : j + 1, :] * dpad[3 - j + k * Q : 3 - j + (k + 1) * Q, :]
        out[k * Q : (k + 1) * Q, :] = g.astype(BF)
        if k == NB - 1:
            last[...] = g[Q - 16 :, :]
    z = jnp.zeros((1, pad.shape[1]), F32)
    d = [dpad[m : m + 1, :] for m in range(3)]
    ws = [w[j : j + 1, :] for j in range(3)]
    corr[...] = jnp.concatenate(
        [z] * 5 + [ws[0] * d[0], ws[1] * d[0] + ws[0] * d[1], ws[2] * d[0] + ws[1] * d[1] + ws[0] * d[2]], axis=0
    )
    dw[...] = jnp.concatenate(sums + [z] * 3, axis=0)


def final_kernel(x, xh, dy, w, b, bh, c, ch, wb, wc, rs, rt, skip, bc, cc, bct, cct, sin, din, logs, sig, rate,
                 yo, gxo, gbo, gco, gdo, toto,
                 pad, dpad, S, sc, gacc, db, dc, qs, ends_s,
                 ybuf, gbuf, bbuf, cbuf, last, corr, halo, tail, gdt, dts, v, ra, rb, part, mid, tot,
                 xs, xr, bs, br, gs, gr, ks, kr, ts, tr, loc, s1, r1, s2, r2, s3, r3):
    pid = pl.program_id(0)
    dp_i = lax.axis_index("dp")
    me, y, seg = place()
    base = seg * NY
    xhi = lax.div(seg, 8)
    z = lax.rem(seg, 8)
    up = lax.rem(seg + 1, NSEG) * NY + y
    down = lax.rem(seg + NSEG - 1, NSEG) * NY + y
    hops = (1, 3, 2)
    peers = [base + lax.rem(y + i, NY) for i in hops]

    def to(d, h, zz, yy):
        return {"dp": d, "sp": h * 32 + zz * 4 + yy}

    along_z = [to(dp_i, xhi, lax.rem(z + i, 8), y) for i in range(1, 8)]
    pos = dp_i * 2 + xhi
    along_x = []
    for i in range(1, 8):
        q = lax.rem(pos + i, 8)
        along_x.append(to(lax.div(q, 2), lax.rem(q, 2), z, y))
    pzy = z * 4 + y
    along_zy = [{"dp": dp_i, "sp": xhi * 32 + lax.rem(pzy + i, 32)} for i in range(1, 32)]

    def lanes(i, wd):
        return pl.ds(pl.multiple_of(i * wd, wd), wd)

    def bulk(i, act):
        for k, hop in enumerate(hops):
            j = lax.rem(y + hop, NY)
            dst_l = pl.ds(pl.multiple_of(y * XW + i * CW, CW), CW)
            act(remote(ybuf.at[pl.ds(pl.multiple_of(j * Q, Q), Q), lanes(i, CW)], yo.at[:, dst_l],
                       xs.at[i, 0, k], xr.at[i, 0, k], peers[k]))
            for rows, cond in ((Q - 16, j == NY - 1), (Q, j != NY - 1)):
                @pl.when(cond)
                def _():
                    act(remote(gbuf.at[pl.ds(pl.multiple_of(j * Q, Q), rows), lanes(i, CW)],
                               gxo.at[pl.ds(0, rows), dst_l], xs.at[i, 1, k], xr.at[i, 1, k], peers[k]))

    def bulk_wait(i):
        src_l = lanes(i, CW)
        for k in range(3):
            remote(ybuf.at[pl.ds(0, Q), src_l], yo.at[:, src_l], xs.at[i, 0, k], xr.at[i, 0, k], peers[k]).wait_recv()
            for rows, cond in ((Q - 16, y == NY - 1), (Q, y != NY - 1)):
                @pl.when(cond)
                def _():
                    remote(gbuf.at[pl.ds(0, rows), src_l], gxo.at[pl.ds(0, rows), src_l],
                           xs.at[i, 1, k], xr.at[i, 1, k], peers[k]).wait_recv()

    def halo_copy(i):
        return remote(corr.at[:, lanes(i, CW)], halo.at[:, lanes(i, CW)], ks.at[i], kr.at[i], down)

    @pl.when(pid == 0)
    def _():
        barrier = pltpu.get_barrier_semaphore()
        for t in along_x + along_zy:
            pl.semaphore_signal(barrier, inc=1, device_id=t, device_id_type=MESH)
        for t in (up, down):
            pl.semaphore_signal(barrier, inc=1, device_id={"sp": t}, device_id_type=MESH)
        pl.semaphore_wait(barrier, 40)
        for k in range(NB):
            sl = slice(k * Q, (k + 1) * Q)
            sc[k] = dot(cc[sl, :], bc[sl, :], 1, 1)
        gacc[...] = jnp.zeros_like(gacc)
        db[...] = jnp.zeros_like(db)
        dc[...] = jnp.zeros_like(dc)
        qs[...] = jnp.zeros_like(qs)
        ends_s[...] = jnp.zeros_like(ends_s)
        v[...] = jnp.zeros_like(v)

    @pl.when(pid > 0)
    def _():
        bulk(pid - 1, lambda cp: cp.start())
        halo_copy(pid - 1).start()

    here = lanes(pid, CW)
    fill(pad, xh, x)
    wx = w[...]
    S[0] = join(sin)
    for k in range(NB):
        sl = slice(k * Q, (k + 1) * Q)
        s = conv_rows(pad, wx, wx[4:5, :], k)
        xc = (s * sigmoid(s)).astype(BF).astype(F32)
        r = spread(rs[0, sl, 0:4])
        st = spread(rs[0, sl, 4:8])
        re = r[Q - 1 : Q, :]
        wt = (xc * (st * jnp.exp(re - r))).astype(BF)
        S[k + 1] = jnp.exp(re) * S[k] + dot(bct[:, sl], wt, 1, 0)

    D = join(din)
    causal = lax.broadcasted_iota(jnp.int32, (Q, Q), 0) >= lax.broadcasted_iota(jnp.int32, (Q, Q), 1)
    low = lax.broadcasted_iota(jnp.int32, (Q, 128), 1) < 64
    er = lax.broadcasted_iota(jnp.int32, (CW, 128), 0) // 64 + pid * (CW // 64) + y * (XW // 64)
    pick = (lax.broadcasted_iota(jnp.int32, (CW, 128), 1) == er).astype(BF)
    ends = []
    for k in reversed(range(NB)):
        sl = slice(k * Q, (k + 1) * Q)
        s = conv_rows(pad, wx, wx[4:5, :], k)
        sg = sigmoid(s)
        xcb = (s * sg).astype(BF)
        xc = xcb.astype(F32)
        dyb = dy[sl, :]
        dyf = dyb.astype(F32)
        rc = rs[0, sl, 0:4]
        r = spread(rc)
        st = spread(rs[0, sl, 4:8])
        re = r[Q - 1 : Q, :]
        er_ = jnp.exp(r)
        ee = jnp.exp(re - r)
        ub = (xc * st).astype(BF)
        wt = (xc * (st * ee)).astype(BF)
        vv = (dyf * er_).astype(BF)
        Sb = S[k].astype(BF)
        Db = D.astype(BF)
        ends.append(jnp.sum(D * S[k + 1], axis=0, keepdims=True))
        ya = er_ * dot(cc[sl, :], Sb, 1, 0)
        du = ee * dot(bc[sl, :], Db, 1, 0)
        db[sl, :] += dot(wt, Db, 1, 1)
        dc[sl, :] += dot(vv, Sb, 1, 1)
        yw, dw_ = [], []
        g = sc[k]
        acc = gacc[k]
        zero = jnp.zeros((Q, 128), BF)
        for p in range(CW // 128):
            ls = []
            for h in (2 * p, 2 * p + 1):
                gap = rc[:, h : h + 1] - rt[0, h : h + 1, sl]
                ls.append(jnp.exp(jnp.where(causal, gap, -1e30)))
            u2 = ub[:, p * 128 : (p + 1) * 128]
            d2 = dyb[:, p * 128 : (p + 1) * 128]
            ublk = jnp.concatenate([jnp.where(low, u2, zero), jnp.where(low, zero, u2)], axis=0)
            dblk = jnp.concatenate([jnp.where(low, d2, zero), jnp.where(low, zero, d2)], axis=0)
            ms = [(g * l).astype(BF) for l in ls]
            yw.append(dot(jnp.concatenate(ms, axis=1), ublk, 1, 0))
            dw_.append(dot(jnp.concatenate(ms, axis=0), dblk, 0, 0))
            dm = dot(d2, ublk, 1, 1)
            acc = acc + dm[:, :Q] * ls[0] + dm[:, Q:] * ls[1]
        gacc[k] = acc
        yin = ya + jnp.concatenate(yw, axis=1)
        du = du + jnp.concatenate(dw_, axis=1)
        sk = skip[0:1, :]
        ybuf[sl, here] = (yin + sk * xc).astype(BF)
        for i, q in enumerate((dyf * yin - ub.astype(F32) * du, xc * du, dyf * xc)):
            parts = pieces(q, 2)
            qs[i, sl, :] += dot(parts[0], pick, 1, 0) + dot(parts[1], pick, 1, 0)
        gx = st * du + sk * dyf
        dpad[sl, :] = gx * (sg * (1.0 + s * (1.0 - sg)))
        D = jnp.exp(re) * D + dot(cct[:, sl], vv, 1, 0)
    for part_e in pieces(jnp.concatenate(ends[::-1] + [jnp.zeros((4, CW), F32)], axis=0), 3):
        ends_s[...] += dot(part_e, pick, 1, 0)
    conv_back(pad, dpad, wx, gbuf.at[:, here], last.at[:, here], corr.at[:, here], v.at[:, here])

    @pl.when(pid == NCH - 1)
    def _():
        for raw, hal, wt, gout, at, acc, other, tr_ in (
            (b, bh, wb, bbuf, XW, db, cc, True),
            (c, ch, wc, cbuf, XW + N, dc, bc, False),
        ):
            fill(pad, hal, raw)
            for k in range(NB):
                sl = slice(k * Q, (k + 1) * Q)
                gk = gacc[k].astype(BF)
                tt = acc[sl, :] + dot(gk, other[sl, :], 0 if tr_ else 1, 0)
                s = conv_rows(pad, wt[...], wt[4:5, :], k)
                sg = sigmoid(s)
                dpad[sl, :] = tt * (sg * (1.0 + s * (1.0 - sg)))
            ln = slice(at, at + N)
            conv_back(pad, dpad, wt[...], gout, last.at[:, ln], corr.at[:, ln], v.at[:, ln])
        after = (lax.broadcasted_iota(jnp.int32, (Q, Q), 0) <= lax.broadcasted_iota(jnp.int32, (Q, Q), 1)).astype(BF)
        own = lax.broadcasted_iota(jnp.int32, (1, 128), 1) // (XW // 64) == y
        sums = [jnp.zeros((1, 128), F32) for _ in range(3)]
        for k in range(NB):
            sl = slice(k * Q, (k + 1) * Q)
            dlog = ends_s[k : k + 1, :] + sum(dot(after, p, 1, 0) for p in pieces(qs[0, sl, :], 3))
            draw = (qs[1, sl, :] - dlog * rate[0:1, :]) * sig[sl, :]
            gdt[sl, :] = draw.astype(BF)
            for i, q in enumerate((dlog * logs[sl, :], draw, qs[2, sl, :])):
                sums[i] = sums[i] + jnp.sum(q, axis=0, keepdims=True)
        v[:, WW : WW + 128] = jnp.where(own, jnp.concatenate(sums + [jnp.zeros((5, 128), F32)], axis=0), 0.0)

        bulk(NCH - 1, lambda cp: cp.start())
        for i in range(NCH - 1, NCH + 2):
            halo_copy(i).start()

        def side(act):
            for k, hop in enumerate(hops):
                j = lax.rem(y + hop, NY)
                act(remote(gdt.at[pl.ds(pl.multiple_of(j * Q, Q), Q), :], dts.at[k], gs.at[k], gr.at[k], peers[k]))
                for n, (src, dst) in enumerate(((bbuf, gbo), (cbuf, gco))):
                    for rows, cond in ((Q - 16, j == NY - 1), (Q, j != NY - 1)):
                        @pl.when(cond)
                        def _():
                            act(remote(src.at[pl.ds(pl.multiple_of(j * Q, Q), rows), :],
                                       dst.at[pl.ds(0, rows), lanes(y, N)], bs.at[n, k], br.at[n, k], peers[k]))

        side(lambda cp: cp.start())

        def send(src, dst, sa, sb, t):
            cp = pltpu.make_async_remote_copy(src_ref=src, dst_ref=dst, send_sem=sa, recv_sem=sb,
                                              device_id=t, device_id_type=MESH)
            cp.start()
            return cp

        first = [send(v.at[:, lanes(lax.rem(z + i + 1, 8), ZW)], ra.at[z], s1.at[i], r1.at[i], t)
                 for i, t in enumerate(along_z)]
        mine = pl.ds(pl.multiple_of(y * Q, Q), Q)
        y_own = pltpu.make_async_copy(ybuf.at[mine, :], yo.at[:, lanes(y, XW)], loc.at[0])
        y_own.start()
        for i in range(NCH + 2):
            halo_copy(i).wait_recv()

        @pl.when(seg == NSEG - 1)
        def _():
            tail[...] = last[...].astype(BF)

        @pl.when(seg != NSEG - 1)
        def _():
            tail[0:8, :] = last[0:8, :].astype(BF)
            tail[8:16, :] = (last[8:16, :] + halo[...]).astype(BF)

        tails = ((0, XW, gxo), (XW, N, gbo), (XW + N, N, gco))

        def tail_copy(n, k):
            at, wd, dst = tails[n]
            return remote(tail.at[:, pl.ds(at, wd)], dst.at[pl.ds(Q - 16, 16), lanes(y, wd)],
                          ts.at[n, k], tr.at[n, k], base + NY - 1)

        for k, hop in enumerate(hops):
            @pl.when(lax.rem(y + hop, NY) == NY - 1)
            def _():
                for n in range(3):
                    tail_copy(n, k).start()

        @pl.when(y == NY - 1)
        def _():
            gbuf[T - 16 :, :] = tail[:, :XW]
            bbuf[T - 16 :, :] = tail[:, XW : XW + N]
            cbuf[T - 16 :, :] = tail[:, XW + N :]

        ra[z] = v[:, lanes(z, ZW)]
        for cp in first:
            cp.wait()
        t1 = ra[0]
        for i in range(1, 8):
            t1 = t1 + ra[i]
        part[...] = t1
        rb[pos] = t1
        second = [send(part, rb.at[pos], s2.at[i], r2.at[i], t) for i, t in enumerate(along_x)]
        owns = [y_own]
        for n, (src, dst, wd) in enumerate(((gbuf, gxo, XW), (bbuf, gbo, N), (cbuf, gco, N))):
            o = pltpu.make_async_copy(src.at[mine, :], dst.at[:, lanes(y, wd)], loc.at[1 + n])
            o.start()
            owns.append(o)
        for cp in second:
            cp.wait()
        t2 = rb[0]
        for i in range(1, 8):
            t2 = t2 + rb[i]
        mid[...] = t2
        zl = lanes(z, ZW)
        tot[y, :, zl] = t2
        third = [send(mid, tot.at[y, :, zl], s3.at[i], r3.at[i], t) for i, t in enumerate(along_zy)]
        for cp in third:
            cp.wait()
        toto[...] = tot[...]
        side(lambda cp: cp.wait_send())
        for k in range(3):
            remote(gdt.at[pl.ds(0, Q), :], dts.at[k], gs.at[k], gr.at[k], peers[k]).wait_recv()
            for n, (src, dst) in enumerate(((bbuf, gbo), (cbuf, gco))):
                for rows, cond in ((Q - 16, y == NY - 1), (Q, y != NY - 1)):
                    @pl.when(cond)
                    def _():
                        remote(src.at[pl.ds(0, rows), :], dst.at[pl.ds(0, rows), pl.ds(0, N)],
                               bs.at[n, k], br.at[n, k], peers[k]).wait_recv()
        gd = gdt[mine, :].astype(F32)
        for k in range(3):
            gd = gd + dts[k].astype(F32)
        gdo[...] = gd.astype(BF)
        for o in owns:
            o.wait()
        for i in range(NCH + 2):
            halo_copy(i).wait_send()

        def drain(i, carry):
            bulk(i, lambda cp: cp.wait_send())
            bulk_wait(i)
            return carry

        lax.fori_loop(0, NCH, drain, 0)
        for k, hop in enumerate(hops):
            @pl.when(lax.rem(y + hop, NY) == NY - 1)
            def _():
                for n in range(3):
                    tail_copy(n, k).wait_send()

            @pl.when(y == NY - 1)
            def _():
                for n in range(3):
                    tail_copy(n, k).wait_recv()


def finals(*args):
    s = jax.ShapeDtypeStruct
    V = pltpu.VMEM
    dma = pltpu.SemaphoreType.DMA
    return pl.pallas_call(
        final_kernel,
        name="outputs_and_gradients",
        grid=(NCH,),
        out_shape=[s((Q, NY * XW), BF), s((Q, NY * XW), BF), s((Q, NY * N), BF), s((Q, NY * N), BF),
                   s((Q, 128), BF), s((NY, 8, VW), F32)],
        in_specs=[chunked(T), chunked(HALO), chunked(T), chunked(8), whole(T, N), whole(HALO, N),
                  whole(T, N), whole(HALO, N), whole(8, N), whole(8, N), RS, RT, chunked(8),
                  whole(T, N), whole(T, N), whole(N, T), whole(N, T), PIECES, PIECES,
                  whole(T, 128), whole(T, 128), whole(8, 128)],
        out_specs=[ANY] * 4 + [whole(Q, 128), whole(NY, 8, VW)],
        scratch_shapes=[
            V((T + 8, CW), F32), V((T + 8, CW), F32), V((NB + 1, N, CW), F32),
            V((NB, Q, Q), F32), V((NB, Q, Q), F32), V((T, N), F32), V((T, N), F32),
            V((3, T, 128), F32), V((8, 128), F32),
            V((T, XW), BF), V((T, XW), BF), V((T, N), BF), V((T, N), BF),
            V((16, WW), F32), V((8, WW), F32), V((8, WW), F32), V((16, WW), BF),
            V((T, 128), BF), V((3, Q, 128), BF),
            V((8, VW), F32), V((8, 8, ZW), F32), V((8, 8, ZW), F32), V((8, ZW), F32), V((8, ZW), F32),
            V((NY, 8, VW), F32),
            dma((NCH, 2, 3)), dma((NCH, 2, 3)), dma((2, 3)), dma((2, 3)), dma((3,)), dma((3,)),
            dma((NCH + 2,)), dma((NCH + 2,)), dma((3, 3)), dma((3, 3)), dma((4,)),
            dma((7,)), dma((7,)), dma((7,)), dma((7,)), dma((31,)), dma((31,)),
        ],
        compiler_params=pltpu.CompilerParams(collective_id=2, has_side_effects=True, vmem_limit_bytes=VLIM),
    )(*args)


def per_device(ssm_input, b_input, c_input, dt_input, conv_weight, conv_bias, a_log, dt_bias, skip_gain, grad_out):
    me = lax.axis_index("sp")
    y = lax.rem(me, NY)
    seg = lax.div(me, NY)
    x, dy, b, c, dt, xh, bh, ch = bring(ssm_input[0], grad_out[0], b_input[0], c_input[0], dt_input[0])
    first = seg == 0
    xh, bh, ch = [jnp.where(first, jnp.zeros_like(h), h) for h in (xh, bh, ch)]
    taps = jnp.concatenate([conv_weight, conv_bias[None], jnp.zeros((3, conv_weight.shape[1]), F32)], 0)
    w = lax.dynamic_slice_in_dim(taps, y * XW, XW, 1)
    wb = lax.dynamic_slice_in_dim(taps, NY * XW + y * N, N, 1)
    wc = lax.dynamic_slice_in_dim(taps, NY * (XW + N) + y * N, N, 1)
    heads = XW // 64

    def own(v):
        return lax.dynamic_slice_in_dim(v, y * heads, heads, 0)

    rate = jnp.exp(own(a_log))
    raw = lax.dynamic_slice_in_dim(dt, y * heads, heads, 1).astype(F32) + own(dt_bias)[None, :]
    step = jax.nn.softplus(raw)
    logs = -step * rate[None, :]
    tril = (jnp.arange(Q)[:, None] >= jnp.arange(Q)[None, :]).astype(F32)
    run = jnp.einsum("ts,ksh->kth", tril, logs.reshape(NB, Q, heads), precision=HP)
    whole_decay = jnp.exp(run[:, -1, :].sum(0))
    run = run.reshape(T, heads)
    per = CW // 64
    rs = jnp.concatenate([run.reshape(T, NCH, per), step.reshape(T, NCH, per)], 2).transpose(1, 0, 2)
    rt = jnp.pad(run.reshape(T, NCH, per).transpose(1, 2, 0), ((0, 0), (0, 8 - per), (0, 0)))
    skip = jnp.broadcast_to(jnp.repeat(own(skip_gain), 64)[None, :], (8, XW))
    lanes = jnp.repeat(whole_decay, 64).reshape(NCH, 1, 2, 128)
    decay = jnp.broadcast_to(lanes, (NCH, 2, 2, 128)).reshape(NPIECE, 1, 128)
    decay = jnp.broadcast_to(decay, (NPIECE, 8, 128))
    bc, cc, bct, cct, sl, dl = local_states(x, xh, dy, w, b, bh, c, ch, wb, wc, rs)
    sin, din = chains(sl, dl, decay)
    full = dt.astype(F32) + dt_bias[None, :]
    full_rate = jnp.exp(a_log)
    yo, gxo, gbo, gco, gdo, tot = finals(
        x, xh, dy, w, b, bh, c, ch, wb, wc, rs, rt, skip, bc, cc, bct, cct, sin, din,
        -jax.nn.softplus(full) * full_rate[None, :], jax.nn.sigmoid(full),
        jnp.broadcast_to(full_rate[None, :], (8, 128)),
    )
    grads = tot[:, :5, :].transpose(1, 0, 2)
    gw = jnp.concatenate(
        [grads[:, :, :XW].reshape(5, -1), grads[:, :, XW : XW + N].reshape(5, -1), grads[:, :, XW + N : WW].reshape(5, -1)], 1
    )
    hsum = tot[:, :3, WW : WW + 128].sum(0)
    hsum = lax.dynamic_slice_in_dim(hsum, me * 2, 2, 1)
    return (yo[None], gxo[None], gbo[None], gco[None], gdo[None], gw[:4], gw[4], hsum)


def solution(mesh):
    row = P("dp", "sp", None)
    return jax.shard_map(
        per_device, mesh=mesh,
        in_specs=(row, row, row, row, P(), P(), P(), P(), P(), row),
        out_specs=(row, row, row, row, row, P(), P(), P(None, "sp")),
        check_vma=False,
    )
```
